32 devices in a mesh: group: 2 (over x), tile: 16 (over z, y, core).
Axes of the slice: x: 2, y: 2, z: 4, core: 2. Of those that a mesh axis runs over, the one named last changes fastest.
Arguments:
- hadamard: int32 [128, 1152], P(None, 'tile'), may hold values from -1 to 1, as said below
- stroke: float32 [2304], P(('group', 'tile')), parts along dimension 0, may hold values from 0.3 to 1
- influence: bfloat16 [3, 2304, 8192], P(None, ('group', 'tile')), parts along dimension 1, may hold values from -0.4375 to 0.4375
- amplitude: float32 [1024, 16, 16], P(('group', 'tile')), parts along dimension 0, may hold values from 0.3 to 1
- aberration: float32 [1024, 16, 16], P(('group', 'tile')), parts along dimension 0, may hold values from -3 to 3
- valid_mask: int32 [1024], P(('group', 'tile')), parts along dimension 0, may hold values from 0 to 1, as said below
Outputs:
- imat: float32 [2304, 2, 512], P(('group', 'tile')), parts along dimension 0
The draws below stay inside these ranges and needn't reach their ends.
There are 2 independent parts, one for each index of `group`. The reference program is written for one: setup_inputs(seed, part) draws one part's arguments, and reference() takes and returns one part's arrays. A program takes and returns all parts, laid end to end along the dimension named above; an argument that names none is the same for every part. Nothing has to cross between parts.
Inputs may be any that keep to these rules, and one draw needn't show every extreme that they name: `hadamard`: each column is one column of a Sylvester-Hadamard matrix whose order is the least power of two not below 1152, restricted to 128 distinct rows of it; different actuators take different columns. `valid_mask`: every pupil tile of 32 subapertures holds at least one valid subaperture.
All inputs are finite; a program needn't handle non-finite values.
Results may differ from the reference program's by a relative error of at most 0.0055.
Values may be sent and summed in bfloat16 or wider, within the bound.
No kernel may reach another device: no remote copies, remote signals or barrier semaphores. Data moves between devices by JAX's collectives and lax.ppermute only.
A program may use at most 128 MiB of HBM per device.

```python
import math
import jax
import jax.numpy as jnp
from jax import lax

PAT = 128
ACT_DEV = 72
SUB_DEV = 32
SAMP = 16
PIX = 16
ACTS = 1152
SUBS = 512
PTS = 8192
N_TILE = 16


def draw_hadamard(key, part):
    order_bits = max(1, (ACTS - 1).bit_length())
    order = 2 ** order_bits
    row_pick = jax.random.permutation(jax.random.fold_in(key, 17), order)[:PAT].astype(jnp.int32)
    column_pick = jax.random.permutation(jax.random.fold_in(key, 29), order)[:ACTS].astype(jnp.int32)
    shared = jnp.bitwise_and(row_pick[:, None], column_pick[None, :])
    parity = jnp.zeros((PAT, ACTS), jnp.int32)
    for place in range(order_bits):
        parity = jnp.bitwise_xor(parity, jnp.bitwise_and(jnp.right_shift(shared, place), 1))
    return (1 - 2 * parity).astype(jnp.int32)


def draw_valid_mask(key, part):
    base_draw = jax.random.randint(jax.random.fold_in(key, 41), (N_TILE, SUB_DEV), 0, 4)
    base_mask = (base_draw < 3).astype(jnp.int32)
    forced_place = jax.random.randint(jax.random.fold_in(key, 53), (N_TILE, 1), 0, SUB_DEV)
    places = jnp.arange(SUB_DEV, dtype=jnp.int32)[None, :]
    forced = (places == forced_place).astype(jnp.int32)
    return jnp.maximum(base_mask, forced).reshape(SUBS).astype(jnp.int32)


def block_scale(stream_key, extent, shards, low, largest):
    factor_of, own = 1.0, jax.random.fold_in(stream_key, 6)
    for axis_at, shards_of in shards:
        draws = jnp.exp(jax.random.uniform(jax.random.fold_in(own, axis_at), (shards_of,), jnp.float32, low / len(shards), largest / len(shards)))
        factor_of = factor_of * jnp.repeat(draws, extent[axis_at] // shards_of).reshape([-1 if axis == axis_at else 1 for axis in range(len(extent))])
    return factor_of


def normal_values(own_key, dims, width, most, pieces=(), kind=jnp.bfloat16):
    level = block_scale(own_key, dims, pieces, -0.22, 0.18) if pieces else 1.0
    drawn = jax.random.normal(own_key, dims, jnp.float32) * width * level
    return jnp.minimum(jnp.maximum(drawn, -most), most).astype(kind)


def setup_inputs(seed: int = 0, part: int = 0) -> dict:
    splits = jax.random.split(jax.random.key(seed), 7)
    own_keys = jax.random.split(jax.random.fold_in(splits[6], part), 7)
    return {
        "hadamard": draw_hadamard(jax.random.fold_in(splits[6], 71), part),
        "stroke": jnp.clip(jnp.exp(math.log(1.0) - 1.2039728 * jax.random.uniform(own_keys[1], (ACTS,), jnp.float32) ** block_scale(own_keys[1], (ACTS,), ((0, 16),), -0.2, 0.2)), 0.3, 1.0),
        "influence": normal_values(own_keys[2], (3, ACTS, PTS), (3 * ACT_DEV) ** -0.5, 0.4375, ((1, 16),)),
        "amplitude": jnp.clip(jnp.exp(math.log(1.0) - 1.2039728 * jax.random.uniform(own_keys[3], (SUBS, SAMP, SAMP), jnp.float32) ** block_scale(own_keys[3], (SUBS, SAMP, SAMP), ((0, 16),), -0.2, 0.2)), 0.3, 1.0),
        "aberration": normal_values(own_keys[4], (SUBS, SAMP, SAMP), 0.5, 3.0, ((0, 16),), jnp.float32),
        "valid_mask": draw_valid_mask(jax.random.fold_in(jax.random.fold_in(splits[6], part), 71), part),
    }


HIGHEST = lax.Precision.HIGHEST


def transform_tables(samples, pixels):
    freqs = jnp.arange(pixels, dtype=jnp.float32) - pixels / 2.0
    places = jnp.arange(samples, dtype=jnp.float32)
    angle = 2.0 * jnp.pi * freqs[:, None] * places[None, :] / (2.0 * samples)
    return jnp.cos(angle), -jnp.sin(angle)


def kron_tables(samples, pixels):
    table_real, table_imag = transform_tables(samples, pixels)
    kron_real = jnp.kron(table_real, table_real) - jnp.kron(table_imag, table_imag)
    kron_imag = jnp.kron(table_real, table_imag) + jnp.kron(table_imag, table_real)
    upper = jnp.concatenate([kron_real.T, kron_imag.T], axis=1)
    lower = jnp.concatenate([-kron_imag.T, kron_real.T], axis=1)
    transform = jnp.concatenate([upper, lower], axis=0)
    centre = jnp.arange(pixels, dtype=jnp.float32) - (pixels - 1) / 2.0
    along_u = jnp.repeat(centre, pixels)
    along_v = jnp.tile(centre, pixels)
    moments = jnp.stack([jnp.ones_like(along_u), along_u, along_v], axis=1)
    return transform, moments


def spot_slopes(phase_map, amplitude, aberration, valid_mask):
    patterns, sub_count, samples = phase_map.shape[0], phase_map.shape[1], phase_map.shape[2]
    flat = samples * samples
    transform, moments = kron_tables(samples, PIX)
    half = PIX * PIX
    phase_rows = phase_map.reshape(patterns, sub_count, flat)
    amp_rows = amplitude.reshape(sub_count, flat)[None]
    abe_rows = aberration.reshape(sub_count, flat)[None]
    results = []
    for pattern_sign in (1.0, -1.0):
        angles = abe_rows + pattern_sign * phase_rows
        field = jnp.concatenate([amp_rows * jnp.cos(angles), amp_rows * jnp.sin(angles)], axis=2)
        focal = jnp.dot(field.reshape(patterns * sub_count, 2 * flat), transform, precision=HIGHEST)
        intensity = focal[:, :half] * focal[:, :half] + focal[:, half:] * focal[:, half:]
        sums = jnp.dot(intensity, moments, precision=HIGHEST)
        centroid_x = sums[:, 1] / sums[:, 0]
        centroid_y = sums[:, 2] / sums[:, 0]
        results.append(jnp.stack([centroid_x, centroid_y], axis=1).reshape(patterns, sub_count, 2).transpose(0, 2, 1))
    weights = valid_mask.astype(jnp.float32)[None, None, :]
    return ((results[0] - results[1]) * 0.5 * weights).astype(jnp.bfloat16)


def reference(hadamard, stroke, influence, amplitude, aberration, valid_mask):
    commands = (stroke[None, :] * hadamard.astype(jnp.float32)).astype(jnp.bfloat16)

    def one_tile(tile_index):
        phase_map = jnp.zeros((PAT, PTS), jnp.float32)
        for offset in range(3):
            source = tile_index + 1 - offset
            inside = (source >= 0) & (source < N_TILE)
            clipped = jnp.clip(source, 0, N_TILE - 1).astype(jnp.int32)
            block_cmds = lax.dynamic_slice_in_dim(commands, clipped * ACT_DEV, ACT_DEV, 1)
            block_infl = lax.dynamic_slice_in_dim(influence[offset], clipped * ACT_DEV, ACT_DEV, 0)
            term = jnp.dot(block_cmds, block_infl, preferred_element_type=jnp.float32).astype(jnp.bfloat16)
            term = lax.optimization_barrier(term).astype(jnp.float32)
            phase_map = phase_map + jnp.where(inside, term, jnp.zeros_like(term))
        first = (tile_index * SUB_DEV).astype(jnp.int32)
        amp_tile = lax.dynamic_slice_in_dim(amplitude, first, SUB_DEV, 0)
        abe_tile = lax.dynamic_slice_in_dim(aberration, first, SUB_DEV, 0)
        mask_tile = lax.dynamic_slice_in_dim(valid_mask, first, SUB_DEV, 0)
        return spot_slopes(phase_map.reshape(PAT, SUB_DEV, SAMP, SAMP), amp_tile, abe_tile, mask_tile)

    per_tile = lax.map(one_tile, jnp.arange(N_TILE, dtype=jnp.int32))
    slopes = jnp.transpose(per_tile, (1, 2, 0, 3)).reshape(PAT, 2 * SUBS)
    summed = jnp.dot(hadamard.astype(jnp.bfloat16).T, slopes, preferred_element_type=jnp.float32)
    return summed.reshape(ACTS, 2, SUBS) / (PAT * stroke)[:, None, None]
```

```python
import math

import jax
import jax.numpy as jnp
import numpy as np
from jax import lax
from jax.experimental import pallas as pl
from jax.experimental.pallas import tpu as pltpu
from jax.sharding import PartitionSpec as P

PIX = 16


def half_turn_tables():
    nodes = 0.125 * (1.0 - np.cos(np.pi * (np.arange(200) + 0.5) / 200))
    r = np.sqrt(nodes)
    sin_fit = np.polynomial.chebyshev.Chebyshev.fit(
        nodes, math.sqrt(2) * np.sin(np.pi * r) / r, 4, domain=[0, 0.25]
    ).convert(kind=np.polynomial.Polynomial)
    cos_fit = np.polynomial.chebyshev.Chebyshev.fit(
        nodes, math.sqrt(2) * np.cos(np.pi * r), 5, domain=[0, 0.25]
    ).convert(kind=np.polynomial.Polynomial)
    return [float(c) for c in sin_fit.coef], [float(c) for c in cos_fit.coef]


SIN_FIT, COS_FIT = half_turn_tables()


def horner(coefs, z):
    value = z * coefs[-1] + coefs[-2]
    for c in coefs[-3::-1]:
        value = value * z + c
    return value


def cos_sin(phase):
    turns = phase * (1.0 / (2.0 * math.pi))
    r = turns - jnp.round(turns)
    z = r * r
    half_sin = horner(SIN_FIT, z) * r
    half_cos = horner(COS_FIT, z)
    return 1.0 - half_sin * half_sin, half_sin * half_cos


def dft_tables(samples, pixels):
    freqs = np.arange(pixels) - pixels / 2.0
    table = np.exp(-2j * np.pi * freqs[:, None] * np.arange(samples)[None, :] / (2.0 * samples))
    full = np.kron(table, table)
    return full.real.astype(np.float32), full.imag.astype(np.float32)


def subaperture_transforms(amplitude, aberration):
    subs, samples = amplitude.shape[0], amplitude.shape[1]
    real, imag = dft_tables(samples, PIX)
    amp = amplitude.reshape(subs, 1, samples * samples)
    abe = aberration.reshape(subs, 1, samples * samples)
    field_re, field_im = amp * jnp.cos(abe), amp * jnp.sin(abe)
    first = jnp.asarray(np.concatenate([real, imag]))[None]
    second = jnp.asarray(np.concatenate([-imag, real]))[None]
    return (first * field_re + second * field_im).astype(jnp.bfloat16)


def spots_kernel(per_step, mask_ref, cmd_a, cmd_b, cmd_c, slab_a, slab_b, slab_c, trans_ref, out_ref, cmds, sums):
    step = pl.program_id(0)
    half = PIX * PIX
    flat = trans_ref.shape[2]

    @pl.when(step == 0)
    def _():
        for k, ref in enumerate((cmd_a, cmd_b, cmd_c)):
            cmds[k] = ref[...].astype(jnp.float32).T.astype(jnp.bfloat16)

    patterns = out_ref.shape[2]
    for s in range(per_step):
        cols = slice(s * flat, (s + 1) * flat)
        phase = None
        for k, ref in enumerate((slab_a, slab_b, slab_c)):
            rows = ref[0, :, cols] if len(ref.shape) == 3 else ref[:, cols]
            term = jnp.dot(cmds[k], rows, preferred_element_type=jnp.float32)
            term = term.astype(jnp.bfloat16).astype(jnp.float32)
            phase = term if phase is None else phase + term
        waves = jnp.concatenate([w.astype(jnp.bfloat16) for w in cos_sin(phase)], axis=0)
        focal = lax.dot_general(
            trans_ref[s], waves, (((1,), (1,)), ((), ())), preferred_element_type=jnp.float32
        )
        ur, vr = focal[:half, :patterns], focal[:half, patterns:]
        ui, vi = focal[half:, :patterns], focal[half:, patterns:]
        even = (ur * ur + ui * ui) + (vr * vr + vi * vi)
        odd = ui * vr - ur * vi
        for k, value in enumerate((even, odd)):
            grid = value.reshape(PIX, PIX // 8, 8, patterns)
            along_u = along_v = None
            for u in range(PIX):
                line = grid[u]
                along_v = line if along_v is None else along_v + line
                total = line[0] + line[1]
                moved = total * (u - (PIX - 1) / 2.0)
                along_u = moved if along_u is None else along_u + moved
            sums[k, 0, s] = along_v[0] + along_v[1]
            sums[k, 1, s] = along_u
            below = lax.broadcasted_iota(jnp.int32, (8, patterns), 0).astype(jnp.float32)
            lead = -(PIX - 1) / 2.0
            sums[k, 2, s] = along_v[0] * (below + lead) + along_v[1] * (below + (lead + 8))
    total = jnp.sum(sums[...], axis=3)
    even, odd = total[0], 2.0 * total[1]
    scale = 1.0 / ((even[0] + odd[0]) * (even[0] - odd[0]))
    for c in range(2):
        slope = (odd[1 + c] * even[0] - even[1 + c] * odd[0]) * scale
        for s in range(per_step):
            valid = mask_ref[step * per_step + s].astype(jnp.float32)
            out_ref[c, pl.ds(s, 1), :] = (slope[s : s + 1] * valid).astype(out_ref.dtype)


def spot_slopes(mask, cmds, slabs, transform, first, count, per_step):
    half, flat = transform.shape[1], transform.shape[2]
    acts, patterns = cmds[0].shape
    width = per_step * flat
    skip = first // per_step

    def slab_spec(slab, offset):
        if slab.ndim == 3:
            return pl.BlockSpec((1, acts, width), lambda i: (1, 0, i + offset))
        return pl.BlockSpec((acts, width), lambda i: (0, i + offset))

    return pl.pallas_call(
        lambda *refs: spots_kernel(per_step, *refs),
        grid=(count // per_step,),
        in_specs=[pl.BlockSpec(memory_space=pltpu.SMEM)]
        + [pl.BlockSpec((acts, patterns), lambda i: (0, 0))] * 3
        + [slab_spec(slabs[0], skip), slab_spec(slabs[1], skip), slab_spec(slabs[2], 0)]
        + [pl.BlockSpec((per_step, half, flat), lambda i: (i + skip, 0, 0))],
        out_specs=pl.BlockSpec((2, per_step, patterns), lambda i: (0, i, 0)),
        out_shape=jax.ShapeDtypeStruct((2, count, patterns), jnp.bfloat16),
        scratch_shapes=[
            pltpu.VMEM((3, patterns, acts), jnp.bfloat16),
            pltpu.VMEM((2, 3, per_step, 8, patterns), jnp.float32),
        ],
        name="spots",
    )(mask, *cmds, *slabs, transform)


def pairings(count):
    near = [(i, i ^ 1) for i in range(count) if (i ^ 1) < count]
    far = [(i, i + 1 if i % 2 else i - 1) for i in range(count)]
    return near, [(a, b) for a, b in far if 0 <= b < count]


def per_device(hadamard, stroke, influence, amplitude, aberration, valid_mask):
    count = lax.axis_size("tile")
    parity = lax.axis_index("tile") % 2
    patterns, acts = hadamard.shape
    subs = amplitude.shape[0]
    points = influence.shape[2]
    signs = hadamard.T.astype(jnp.float32)
    commands = (stroke[:, None] * signs).astype(jnp.bfloat16)
    near, far = pairings(count)
    far_slab = lax.dynamic_slice_in_dim(influence, 2 * parity, 1, 0)[0]
    near_slab = lax.dynamic_slice_in_dim(influence, 2 - 2 * parity, 1, 0)[0]
    far_sent = lax.ppermute(jnp.concatenate([far_slab, commands], axis=1), "tile", far)
    near_sent = lax.ppermute(jnp.concatenate([near_slab, commands], axis=1), "tile", near)
    transform = subaperture_transforms(amplitude, aberration)
    cmds = (commands, near_sent[:, points:], far_sent[:, points:])
    slopes = spot_slopes(valid_mask, cmds, (influence, near_sent, far_sent), transform, 0, subs, 8)
    gathered = lax.all_gather(slopes, "tile", axis=1, tiled=True)
    summed = jnp.einsum(
        "ap,csp->acs", signs.astype(jnp.bfloat16), gathered, preferred_element_type=jnp.float32
    )
    return summed / (patterns * stroke)[:, None, None]


def solution(mesh):
    placed = (
        P(None, "tile"),
        P(("group", "tile")),
        P(None, ("group", "tile"), None),
        P(("group", "tile"), None, None),
        P(("group", "tile"), None, None),
        P(("group", "tile")),
    )
    return jax.shard_map(
        per_device,
        mesh=mesh,
        in_specs=placed,
        out_specs=P(("group", "tile"), None, None),
        check_vma=False,
    )
```

```python
import math

import jax
import jax.numpy as jnp
import numpy as np
from jax import lax
from jax.experimental import pallas as pl
from jax.experimental.pallas import tpu as pltpu
from jax.sharding import PartitionSpec as P


PIX = 16
LANES = 8
GROUP = 4


def power_fit(values, nodes, degree):
    fit = np.polynomial.chebyshev.Chebyshev.fit(nodes, values, degree, domain=[0, 0.25])
    return [float(c) for c in fit.convert(kind=np.polynomial.Polynomial).coef]


def half_turn_fits():
    nodes = 0.125 * (1.0 - np.cos(np.pi * (np.arange(200) + 0.5) / 200))
    r = np.sqrt(nodes)
    root = math.sqrt(2.0)
    return (
        power_fit(root * np.sin(np.pi * r) / r, nodes, 3),
        power_fit(root * np.cos(np.pi * r), nodes, 4),
    )


SIN_FIT, COS_FIT = half_turn_fits()


def horner(coefs, z):
    value = z * coefs[-1] + coefs[-2]
    for c in coefs[-3::-1]:
        value = value * z + c
    return value


def cos_sin(phase):
    turns = phase * (1.0 / (2.0 * math.pi))
    r = turns - jnp.round(turns)
    z = r * r
    half_sin = horner(SIN_FIT, z) * r
    half_cos = horner(COS_FIT, z)
    return 1.0 - half_sin * half_sin, half_sin * half_cos


def dft_table(samples, pixels):
    freqs = np.arange(pixels) - pixels / 2.0
    table = np.exp(-2j * np.pi * freqs[:, None] * np.arange(samples)[None, :] / (2.0 * samples))
    full = np.kron(table, table)
    return np.concatenate([full.real, full.imag]).astype(np.float32)


def bf16_term(commands, slab):
    term = jnp.dot(commands, slab, preferred_element_type=jnp.float32)
    return term.astype(jnp.bfloat16).astype(jnp.float32)


def turned(ref_value):
    return ref_value.astype(jnp.float32).T.astype(jnp.bfloat16)


def prepare_kernel(
    cmds_ref, near_ref, amp_ref, abe_ref, table_ref, influence, trans_ref, phase_ref, field, own_slab, cmds, arrival
):
    subs, flat = trans_ref.shape[0], trans_ref.shape[2]
    half = trans_ref.shape[1] // 2
    fetch = pltpu.make_async_copy(influence.at[1], own_slab, arrival)
    fetch.start()
    cosine, sine = cos_sin(abe_ref[...])
    field[0] = (amp_ref[...] * cosine).T
    field[1] = (amp_ref[...] * sine).T
    cmds[0] = turned(cmds_ref[...])
    cmds[1] = turned(near_ref[:, subs * flat :])

    def fold(s, carry):
        real, imag = field[0, pl.ds(s, 1), :], field[1, pl.ds(s, 1), :]
        real = jnp.broadcast_to(real, (2 * LANES, flat))
        imag = jnp.broadcast_to(imag, (2 * LANES, flat))
        for row in range(0, half, 2 * LANES):
            upper, lower = table_ref[row : row + 2 * LANES], table_ref[half + row : half + row + 2 * LANES]
            trans_ref[s, row : row + 2 * LANES] = (upper * real - lower * imag).astype(jnp.bfloat16)
            trans_ref[s, half + row : half + row + 2 * LANES] = (lower * real + upper * imag).astype(jnp.bfloat16)
        return carry

    lax.fori_loop(0, subs, fold, 0)
    fetch.wait()

    def add_terms(g, carry):
        for k in range(GROUP):
            s = g * GROUP + k
            cols = pl.ds(pl.multiple_of(s * flat, flat), flat)
            phase_ref[s] = bf16_term(cmds[0], own_slab[:, cols]) + bf16_term(cmds[1], near_ref[:, cols])
        return carry

    lax.fori_loop(0, subs // GROUP, add_terms, 0)


def prepare(commands, near_sent, influence, amplitude, aberration):
    subs, samples = amplitude.shape[0], amplitude.shape[1]
    flat = samples * samples
    acts, patterns = commands.shape
    table = jnp.asarray(dft_table(samples, PIX))
    half = table.shape[0]
    whole = pl.BlockSpec(memory_space=pltpu.VMEM)
    return pl.pallas_call(
        prepare_kernel,
        in_specs=[whole] * 5 + [pl.BlockSpec(memory_space=pl.ANY)],
        out_specs=[whole] * 2,
        out_shape=[
            jax.ShapeDtypeStruct((subs, half, flat), jnp.bfloat16),
            jax.ShapeDtypeStruct((subs, patterns, flat), jnp.float32),
        ],
        scratch_shapes=[
            pltpu.VMEM((2, subs, flat), jnp.float32),
            pltpu.VMEM((acts, subs * flat), jnp.bfloat16),
            pltpu.VMEM((2, patterns, acts), jnp.bfloat16),
            pltpu.SemaphoreType.DMA,
        ],
        compiler_params=pltpu.CompilerParams(vmem_limit_bytes=8 << 20),
        cost_estimate=pl.CostEstimate(flops=10**9, bytes_accessed=8 << 20, transcendentals=0),
        name="prepare",
    )(
        commands,
        near_sent,
        amplitude.reshape(subs, flat).T,
        aberration.reshape(subs, flat).T,
        table,
        influence,
    )


def running_moments(values):
    middle = (PIX - 1) / 2.0
    low, high, steps = values[0][0], values[0][1], None
    for u in range(1, PIX):
        both = low + high
        steps = both if steps is None else steps + both
        low = low + values[u][0]
        high = high + values[u][1]
    total = low + high
    row = lax.broadcasted_iota(jnp.int32, total.shape, 0).astype(jnp.float32)
    return total, total * middle - steps, low * (row - middle) + high * (row + (LANES - middle))


def spots_kernel(first, lead, done, mask_ref, cmds_ref, slab_ref, trans_ref, phase_ref, *refs):
    earlier, refs = refs[:done], refs[done:]
    out_ref, refs = refs[0], refs[1:]
    sums = refs[-1]
    flat = trans_ref.shape[2]
    patterns = out_ref.shape[2]
    count = sums.shape[2]
    if lead:
        cmds = refs[0]
        cmds[...] = turned(cmds_ref[:, count * flat :])
    else:
        cmds = cmds_ref

    def group(g, carry):
        for k in range(GROUP):
            s = g * GROUP + k
            cols = pl.ds(pl.multiple_of(s * flat, flat), flat)
            phase = phase_ref[first + s] + bf16_term(cmds[...], slab_ref[:, cols])
            waves = jnp.concatenate([w.astype(jnp.bfloat16) for w in cos_sin(phase)], axis=0)
            focal = lax.dot_general(
                trans_ref[first + s],
                waves,
                (((1,), (1,)), ((), ())),
                preferred_element_type=jnp.float32,
            )
            lines = focal.reshape(2, PIX, PIX // LANES, LANES, 2 * patterns)
            even, odd = [], []
            for u in range(PIX):
                even.append([])
                odd.append([])
                for v in range(PIX // LANES):
                    ur, vr = lines[0, u, v, :, :patterns], lines[0, u, v, :, patterns:]
                    ui, vi = lines[1, u, v, :, :patterns], lines[1, u, v, :, patterns:]
                    even[u].append((ur * ur + ui * ui) + (vr * vr + vi * vi))
                    odd[u].append(ui * vr - ur * vi)
            for kind, values in enumerate((even, odd)):
                for m, value in enumerate(running_moments(values)):
                    sums[kind, m, s] = value
        return carry

    lax.fori_loop(0, count // GROUP, group, 0)
    total = jnp.sum(sums[...], axis=3)
    even, odd = total[0], 2.0 * total[1]
    scale = 1.0 / ((even[0] + odd[0]) * (even[0] - odd[0]))
    row = lax.broadcasted_iota(jnp.int32, (count, patterns), 0)
    valid = jnp.zeros((count, patterns), jnp.float32)
    for s in range(count):
        valid = jnp.where(row == s, mask_ref[first + s].astype(jnp.float32), valid)
    scale = scale * valid
    for c in range(2):
        slope = ((odd[1 + c] * even[0] - even[1 + c] * odd[0]) * scale).astype(out_ref.dtype)
        pieces = [ref[c] for ref in earlier] + [slope]
        out_ref[c] = jnp.concatenate(pieces, axis=0) if earlier else slope


def spot_slopes(mask, cmds, slab, transform, phase, first, count, earlier):
    acts = slab.shape[0]
    patterns = phase.shape[1]
    lead = cmds is None
    rows = count + sum(part.shape[1] for part in earlier)
    whole = pl.BlockSpec(memory_space=pltpu.VMEM)
    out_shape = [jax.ShapeDtypeStruct((2, rows, patterns), jnp.bfloat16)]
    if lead:
        out_shape.append(jax.ShapeDtypeStruct((patterns, acts), jnp.bfloat16))
    return pl.pallas_call(
        lambda *refs: spots_kernel(first, lead, len(earlier), *refs),
        in_specs=[pl.BlockSpec(memory_space=pltpu.SMEM)] + [whole] * (4 + len(earlier)),
        out_specs=[whole] * len(out_shape),
        out_shape=out_shape,
        scratch_shapes=[pltpu.VMEM((2, 3, count, LANES, patterns), jnp.float32)],
        compiler_params=pltpu.CompilerParams(vmem_limit_bytes=8 << 20),
        cost_estimate=pl.CostEstimate(flops=10**8 * count, bytes_accessed=10**6, transcendentals=0),
        name="spots",
    )(mask, slab if lead else cmds, slab, transform, phase, *earlier)


def decode_kernel(parity_ref, signs_ref, stroke_ref, same_ref, other_ref, out_ref):
    pairs, rows, patterns = same_ref.shape
    acts = signs_ref.shape[0]
    subs = rows // 2
    signs = signs_ref[...].astype(jnp.float32).astype(jnp.bfloat16)
    scale = jnp.broadcast_to(1.0 / (stroke_ref[...] * patterns), (LANES, acts)).T[:, :1]

    def write(even_ref, odd_ref):
        for c in range(2):
            part = slice(c * subs, (c + 1) * subs)
            slopes = jnp.stack([even_ref[:, part, :], odd_ref[:, part, :]], axis=1)
            summed = lax.dot_general(
                signs,
                slopes.reshape(2 * pairs * subs, patterns),
                (((1,), (1,)), ((), ())),
                preferred_element_type=jnp.float32,
            )
            out_ref[:, c, :] = summed * scale

    pl.when(parity_ref[0] == 0)(lambda: write(same_ref, other_ref))
    pl.when(parity_ref[0] == 1)(lambda: write(other_ref, same_ref))


def decode(parity, signs, stroke, same, other):
    pairs, rows, _ = same.shape
    acts = signs.shape[0]
    return pl.pallas_call(
        decode_kernel,
        in_specs=[pl.BlockSpec(memory_space=pltpu.SMEM)] + [pl.BlockSpec(memory_space=pltpu.VMEM)] * 4,
        out_specs=pl.BlockSpec(memory_space=pltpu.VMEM),
        out_shape=jax.ShapeDtypeStruct((acts, 2, pairs * rows), jnp.float32),
        compiler_params=pltpu.CompilerParams(vmem_limit_bytes=8 << 20),
        name="decode",
    )(parity.reshape(1), signs, stroke.reshape(1, acts), same, other)


def pairings(count):
    near = [(i, i ^ 1) for i in range(count) if (i ^ 1) < count]
    far = [(i, i + 1 if i % 2 else i - 1) for i in range(count)]
    return near, [(a, b) for a, b in far if 0 <= b < count]


def chunk_sizes(subs):
    unit = subs // 8
    return [3 * unit, 2 * unit, 2 * unit, unit]


def interaction(hadamard, stroke, influence, amplitude, aberration, valid_mask):
    count = lax.axis_size("tile")
    parity = lax.axis_index("tile") % 2
    acts = stroke.shape[0]
    subs = amplitude.shape[0]
    flat = influence.shape[2] // subs
    near, far = pairings(count)
    sizes = chunk_sizes(subs)
    firsts = [sum(sizes[:k]) for k in range(len(sizes))]
    commands = (stroke[:, None] * hadamard.T.astype(jnp.float32)).astype(jnp.bfloat16)

    def slab_of(offset, first, size):
        return lax.dynamic_slice(influence, (offset, 0, first * flat), (1, acts, size * flat))[0]

    far_slabs = []
    for k, (first, size) in enumerate(zip(firsts, sizes)):
        sent = slab_of(2 * parity, first, size)
        if k == 0:
            sent = jnp.concatenate([sent, commands], axis=1)
        far_slabs.append(lax.ppermute(sent, "tile", far))
    sent = jnp.concatenate([slab_of(2 - 2 * parity, 0, subs), commands], axis=1)
    near_sent = lax.ppermute(sent, "tile", near)
    transform, phase = prepare(commands, near_sent, influence, amplitude, aberration)
    parts, far_cmds = [], None
    for k, (first, size) in enumerate(zip(firsts, sizes)):
        earlier = parts if k == len(sizes) - 1 else []
        found = spot_slopes(valid_mask, far_cmds, far_slabs[k], transform, phase, first, size, earlier)
        parts.append(found[0])
        if k == 0:
            far_cmds = found[1]
    slopes = parts[-1].reshape(2 * subs, -1)
    groups = [list(range(side, count, 2)) for side in range(2)]
    copies = jnp.broadcast_to(slopes, (count // 2, *slopes.shape))
    same = lax.all_to_all(copies, "tile", 0, 0, axis_index_groups=groups)
    other = lax.ppermute(same, "tile", near)
    return decode(parity, hadamard.T, stroke, same, other)


def solution(mesh):
    placed = (
        P(None, "tile"),
        P(("group", "tile")),
        P(None, ("group", "tile"), None),
        P(("group", "tile"), None, None),
        P(("group", "tile"), None, None),
        P(("group", "tile")),
    )
    return jax.shard_map(
        interaction,
        mesh=mesh,
        in_specs=placed,
        out_specs=P(("group", "tile"), None, None),
        check_vma=False,
    )
```

```python
import math

import jax
import jax.numpy as jnp
import numpy as np
from jax import lax
from jax.experimental import pallas as pl
from jax.experimental.pallas import tpu as pltpu
from jax.sharding import PartitionSpec as P


PIX = 16
LANES = 8
GROUP = 4


def power_fit(values, nodes, degree):
    fit = np.polynomial.chebyshev.Chebyshev.fit(nodes, values, degree, domain=[0, 0.25])
    return [float(c) for c in fit.convert(kind=np.polynomial.Polynomial).coef]


def half_turn_fits():
    nodes = 0.125 * (1.0 - np.cos(np.pi * (np.arange(200) + 0.5) / 200))
    r = np.sqrt(nodes)
    root = math.sqrt(2.0)
    return (
        power_fit(root * np.sin(np.pi * r) / r, nodes, 3),
        power_fit(root * np.cos(np.pi * r), nodes, 3),
    )


SIN_FIT, COS_FIT = half_turn_fits()


def horner(coefs, z):
    value = z * coefs[-1] + coefs[-2]
    for c in coefs[-3::-1]:
        value = value * z + c
    return value


def cos_sin(phase):
    turns = phase * (1.0 / (2.0 * math.pi))
    r = turns - jnp.round(turns)
    z = r * r
    half_sin = horner(SIN_FIT, z) * r
    half_cos = horner(COS_FIT, z)
    return 1.0 - half_sin * half_sin, half_sin * half_cos


def dft_table(samples, pixels):
    freqs = np.arange(pixels) - pixels / 2.0
    table = np.exp(-2j * np.pi * freqs[:, None] * np.arange(samples)[None, :] / (2.0 * samples))
    full = np.kron(table, table)
    return np.concatenate([full.real, full.imag]).astype(np.float32)


def bf16_term(commands, slab):
    term = jnp.dot(commands, slab, preferred_element_type=jnp.float32)
    return term.astype(jnp.bfloat16).astype(jnp.float32)


def turned(ref_value):
    return ref_value.astype(jnp.float32).T.astype(jnp.bfloat16)


def prepare_kernel(
    cmds_ref, near_ref, amp_ref, abe_ref, table_ref, influence, trans_ref, phase_ref, field, own_slab, cmds, arrival
):
    subs, flat = trans_ref.shape[0], trans_ref.shape[2]
    half = trans_ref.shape[1] // 2
    fetch = pltpu.make_async_copy(influence.at[1], own_slab, arrival)
    fetch.start()
    cosine, sine = cos_sin(abe_ref[...])
    field[0] = (amp_ref[...] * cosine).T
    field[1] = (amp_ref[...] * sine).T
    cmds[0] = turned(cmds_ref[...])
    cmds[1] = turned(near_ref[:, subs * flat :])

    def fold(s, carry):
        real, imag = field[0, pl.ds(s, 1), :], field[1, pl.ds(s, 1), :]
        real = jnp.broadcast_to(real, (2 * LANES, flat))
        imag = jnp.broadcast_to(imag, (2 * LANES, flat))
        for row in range(0, half, 2 * LANES):
            upper, lower = table_ref[row : row + 2 * LANES], table_ref[half + row : half + row + 2 * LANES]
            trans_ref[s, row : row + 2 * LANES] = (upper * real - lower * imag).astype(jnp.bfloat16)
            trans_ref[s, half + row : half + row + 2 * LANES] = (lower * real + upper * imag).astype(jnp.bfloat16)
        return carry

    lax.fori_loop(0, subs, fold, 0)
    fetch.wait()

    def add_terms(g, carry):
        for k in range(GROUP):
            s = g * GROUP + k
            cols = pl.ds(pl.multiple_of(s * flat, flat), flat)
            phase_ref[s] = bf16_term(cmds[0], own_slab[:, cols]) + bf16_term(cmds[1], near_ref[:, cols])
        return carry

    lax.fori_loop(0, subs // GROUP, add_terms, 0)


def prepare(commands, near_sent, influence, amplitude, aberration):
    subs, samples = amplitude.shape[0], amplitude.shape[1]
    flat = samples * samples
    acts, patterns = commands.shape
    table = jnp.asarray(dft_table(samples, PIX))
    half = table.shape[0]
    whole = pl.BlockSpec(memory_space=pltpu.VMEM)
    return pl.pallas_call(
        prepare_kernel,
        in_specs=[whole] * 5 + [pl.BlockSpec(memory_space=pltpu.HBM)],
        out_specs=[whole] * 2,
        out_shape=[
            jax.ShapeDtypeStruct((subs, half, flat), jnp.bfloat16),
            jax.ShapeDtypeStruct((subs, patterns, flat), jnp.float32),
        ],
        scratch_shapes=[
            pltpu.VMEM((2, subs, flat), jnp.float32),
            pltpu.VMEM((acts, subs * flat), jnp.bfloat16),
            pltpu.VMEM((2, patterns, acts), jnp.bfloat16),
            pltpu.SemaphoreType.DMA,
        ],
        compiler_params=pltpu.CompilerParams(vmem_limit_bytes=8 << 20),
        cost_estimate=pl.CostEstimate(flops=10**9, bytes_accessed=8 << 20, transcendentals=0),
        name="prepare",
    )(
        commands,
        near_sent,
        amplitude.reshape(subs, flat).T,
        aberration.reshape(subs, flat).T,
        table,
        influence,
    )


def running_moments(values):
    middle = (PIX - 1) / 2.0
    low, high, steps = values[0][0], values[0][1], None
    for u in range(1, PIX):
        both = low + high
        steps = both if steps is None else steps + both
        low = low + values[u][0]
        high = high + values[u][1]
    total = low + high
    row = lax.broadcasted_iota(jnp.int32, total.shape, 0).astype(jnp.float32)
    return total, total * middle - steps, low * (row - middle) + high * (row + (LANES - middle))


def spots_kernel(first, lead, done, mask_ref, cmds_ref, slab_ref, trans_ref, phase_ref, *refs):
    earlier, refs = refs[:done], refs[done:]
    out_ref, refs = refs[0], refs[1:]
    sums = refs[-1]
    flat = trans_ref.shape[2]
    patterns = out_ref.shape[2]
    count = sums.shape[2]
    if lead:
        cmds = refs[0]
        cmds[...] = turned(cmds_ref[:, count * flat :])
    else:
        cmds = cmds_ref

    def group(g, carry):
        for k in range(GROUP):
            s = g * GROUP + k
            cols = pl.ds(pl.multiple_of(s * flat, flat), flat)
            phase = phase_ref[first + s] + bf16_term(cmds[...], slab_ref[:, cols])
            waves = jnp.concatenate([w.astype(jnp.bfloat16) for w in cos_sin(phase)], axis=0)
            focal = lax.dot_general(
                trans_ref[first + s],
                waves,
                (((1,), (1,)), ((), ())),
                preferred_element_type=jnp.float32,
            )
            lines = focal.reshape(2, PIX, PIX // LANES, LANES, 2 * patterns)
            even, odd = [], []
            for u in range(PIX):
                even.append([])
                odd.append([])
                for v in range(PIX // LANES):
                    ur, vr = lines[0, u, v, :, :patterns], lines[0, u, v, :, patterns:]
                    ui, vi = lines[1, u, v, :, :patterns], lines[1, u, v, :, patterns:]
                    even[u].append((ur * ur + ui * ui) + (vr * vr + vi * vi))
                    odd[u].append(ui * vr - ur * vi)
            for kind, values in enumerate((even, odd)):
                for m, value in enumerate(running_moments(values)):
                    sums[kind, m, s] = value
        return carry

    lax.fori_loop(0, count // GROUP, group, 0)
    total = jnp.sum(sums[...], axis=3)
    even, odd = total[0], 2.0 * total[1]
    scale = 1.0 / ((even[0] + odd[0]) * (even[0] - odd[0]))
    row = lax.broadcasted_iota(jnp.int32, (count, patterns), 0)
    valid = jnp.zeros((count, patterns), jnp.float32)
    for s in range(count):
        valid = jnp.where(row == s, mask_ref[first + s].astype(jnp.float32), valid)
    scale = scale * valid
    for c in range(2):
        slope = ((odd[1 + c] * even[0] - even[1 + c] * odd[0]) * scale).astype(out_ref.dtype)
        pieces = [ref[c] for ref in earlier] + [slope]
        out_ref[c] = jnp.concatenate(pieces, axis=0) if earlier else slope


def spot_slopes(mask, cmds, slab, transform, phase, first, count, earlier):
    acts = slab.shape[0]
    patterns = phase.shape[1]
    lead = cmds is None
    rows = count + sum(part.shape[1] for part in earlier)
    whole = pl.BlockSpec(memory_space=pltpu.VMEM)
    out_shape = [jax.ShapeDtypeStruct((2, rows, patterns), jnp.bfloat16)]
    if lead:
        out_shape.append(jax.ShapeDtypeStruct((patterns, acts), jnp.bfloat16))
    return pl.pallas_call(
        lambda *refs: spots_kernel(first, lead, len(earlier), *refs),
        in_specs=[pl.BlockSpec(memory_space=pltpu.SMEM)] + [whole] * (4 + len(earlier)),
        out_specs=[whole] * len(out_shape),
        out_shape=out_shape,
        scratch_shapes=[pltpu.VMEM((2, 3, count, LANES, patterns), jnp.float32)],
        compiler_params=pltpu.CompilerParams(vmem_limit_bytes=8 << 20),
        cost_estimate=pl.CostEstimate(flops=10**8 * count, bytes_accessed=10**6, transcendentals=0),
        name="spots",
    )(mask, slab if lead else cmds, slab, transform, phase, *earlier)


def decode_kernel(parity_ref, signs_ref, stroke_ref, same_ref, other_ref, out_ref):
    pairs, rows, patterns = same_ref.shape
    acts = signs_ref.shape[0]
    subs = rows // 2
    signs = signs_ref[...].astype(jnp.float32).astype(jnp.bfloat16)
    scale = jnp.broadcast_to(1.0 / (stroke_ref[...] * patterns), (LANES, acts)).T[:, :1]

    def write(even_ref, odd_ref):
        for c in range(2):
            part = slice(c * subs, (c + 1) * subs)
            slopes = jnp.stack([even_ref[:, part, :], odd_ref[:, part, :]], axis=1)
            summed = lax.dot_general(
                signs,
                slopes.reshape(2 * pairs * subs, patterns),
                (((1,), (1,)), ((), ())),
                preferred_element_type=jnp.float32,
            )
            out_ref[:, c, :] = summed * scale

    pl.when(parity_ref[0] == 0)(lambda: write(same_ref, other_ref))
    pl.when(parity_ref[0] == 1)(lambda: write(other_ref, same_ref))


def decode(parity, signs, stroke, same, other):
    pairs, rows, _ = same.shape
    acts = signs.shape[0]
    return pl.pallas_call(
        decode_kernel,
        in_specs=[pl.BlockSpec(memory_space=pltpu.SMEM)] + [pl.BlockSpec(memory_space=pltpu.VMEM)] * 4,
        out_specs=pl.BlockSpec(memory_space=pltpu.VMEM),
        out_shape=jax.ShapeDtypeStruct((acts, 2, pairs * rows), jnp.float32),
        compiler_params=pltpu.CompilerParams(vmem_limit_bytes=8 << 20),
        name="decode",
    )(parity.reshape(1), signs, stroke.reshape(1, acts), same, other)


def in_hbm(value):
    return pltpu.with_memory_space_constraint(value, pltpu.HBM)


def pack_first_kernel(parity_ref, signs_hbm, stroke_hbm, influence, sent_ref, cmds_ref, signs, stroke, arrivals):
    acts, patterns = cmds_ref.shape
    width = sent_ref.shape[1] - patterns
    moves = (
        (signs_hbm, signs),
        (stroke_hbm, stroke),
        (influence.at[2 * parity_ref[0], :, pl.ds(0, width)], sent_ref.at[:, pl.ds(0, width)]),
    )
    fetches = [pltpu.make_async_copy(*move, arrivals.at[k]) for k, move in enumerate(moves)]
    for fetch in fetches:
        fetch.start()
    fetches[0].wait()
    fetches[1].wait()
    column = jnp.broadcast_to(stroke[...][None, :], (LANES, acts)).T[:, :1]
    commands = (column * signs[...].astype(jnp.float32)).astype(jnp.bfloat16)
    cmds_ref[...] = commands
    sent_ref[:, width:] = commands
    fetches[2].wait()


def pack_first(parity, signs, stroke, influence, width):
    acts, patterns = signs.shape
    whole, far_off = pl.BlockSpec(memory_space=pltpu.VMEM), pl.BlockSpec(memory_space=pltpu.HBM)
    return pl.pallas_call(
        pack_first_kernel,
        in_specs=[pl.BlockSpec(memory_space=pltpu.SMEM)] + [far_off] * 3,
        out_specs=[whole] * 2,
        out_shape=[
            jax.ShapeDtypeStruct((acts, width + patterns), jnp.bfloat16),
            jax.ShapeDtypeStruct((acts, patterns), jnp.bfloat16),
        ],
        scratch_shapes=[
            pltpu.VMEM((acts, patterns), jnp.int32),
            pltpu.VMEM((acts,), jnp.float32),
            pltpu.SemaphoreType.DMA((3,)),
        ],
        compiler_params=pltpu.CompilerParams(vmem_limit_bytes=8 << 20),
        name="pack_first",
    )(parity.reshape(1), signs, stroke, influence)


def pack_rest_kernel(parity_ref, cmds_ref, influence, *refs):
    pieces, near_ref, arrivals = refs[:-2], refs[-2], refs[-1]
    points = influence.shape[2]
    far_row, near_row = 2 * parity_ref[0], 2 - 2 * parity_ref[0]
    fetches = [
        pltpu.make_async_copy(influence.at[near_row], near_ref.at[:, pl.ds(0, points)], arrivals.at[0])
    ]
    first = points - sum(ref.shape[1] for ref in pieces)
    for k, ref in enumerate(pieces):
        source = influence.at[far_row, :, pl.ds(first, ref.shape[1])]
        fetches.append(pltpu.make_async_copy(source, ref, arrivals.at[k + 1]))
        first += ref.shape[1]
    for fetch in fetches:
        fetch.start()
    near_ref[:, points:] = cmds_ref[...]
    for fetch in fetches:
        fetch.wait()


def pack_rest(parity, commands, influence, widths):
    acts, patterns = commands.shape
    whole = pl.BlockSpec(memory_space=pltpu.VMEM)
    shapes = [(acts, width) for width in widths] + [(acts, influence.shape[2] + patterns)]
    return pl.pallas_call(
        pack_rest_kernel,
        in_specs=[pl.BlockSpec(memory_space=pltpu.SMEM), whole, pl.BlockSpec(memory_space=pltpu.HBM)],
        out_specs=[whole] * len(shapes),
        out_shape=[jax.ShapeDtypeStruct(shape, jnp.bfloat16) for shape in shapes],
        scratch_shapes=[pltpu.SemaphoreType.DMA((len(shapes),))],
        compiler_params=pltpu.CompilerParams(vmem_limit_bytes=8 << 20),
        name="pack_rest",
    )(parity.reshape(1), commands, influence)


def pairings(count):
    near = [(i, i ^ 1) for i in range(count) if (i ^ 1) < count]
    far = [(i, i + 1 if i % 2 else i - 1) for i in range(count)]
    return near, [(a, b) for a, b in far if 0 <= b < count]


def chunk_sizes(subs):
    unit = subs // 8
    return [k * unit for k in (2, 2, 2, 2)]


def interaction(hadamard, stroke, influence, amplitude, aberration, valid_mask):
    count = lax.axis_size("tile")
    parity = lax.axis_index("tile") % 2
    subs = amplitude.shape[0]
    flat = influence.shape[2] // subs
    near, far = pairings(count)
    influence = in_hbm(influence)
    sizes = chunk_sizes(subs)
    firsts = [sum(sizes[:k]) for k in range(len(sizes))]
    widths = [size * flat for size in sizes]
    first_sent, commands = pack_first(parity, in_hbm(hadamard.T), in_hbm(stroke), influence, widths[0])
    far_slabs = [lax.ppermute(first_sent, "tile", far)]
    *rest, near_slab = pack_rest(parity, commands, influence, widths[1:])
    near_sent = lax.ppermute(near_slab, "tile", near)
    for piece in rest:
        far_slabs.append(lax.ppermute(piece, "tile", far))
    transform, phase = prepare(commands, near_sent, influence, amplitude, aberration)
    parts, far_cmds = [], None
    for k, (first, size) in enumerate(zip(firsts, sizes)):
        earlier = parts[-1:]
        found = spot_slopes(valid_mask, far_cmds, far_slabs[k], transform, phase, first, size, earlier)
        parts.append(found[0])
        if k == 0:
            far_cmds = found[1]
    slopes = parts[-1].reshape(2 * subs, -1)
    groups = [list(range(side, count, 2)) for side in range(2)]
    copies = jnp.broadcast_to(slopes, (count // 2, *slopes.shape))
    same = lax.all_to_all(copies, "tile", 0, 0, axis_index_groups=groups)
    other = lax.ppermute(same, "tile", near)
    return decode(parity, hadamard.T, stroke, same, other)


def solution(mesh):
    placed = (
        P(None, "tile"),
        P(("group", "tile")),
        P(None, ("group", "tile"), None),
        P(("group", "tile"), None, None),
        P(("group", "tile"), None, None),
        P(("group", "tile")),
    )
    return jax.shard_map(
        interaction,
        mesh=mesh,
        in_specs=placed,
        out_specs=P(("group", "tile"), None, None),
        check_vma=False,
    )
```

```python
import math

import jax
import jax.numpy as jnp
import numpy as np
from jax import lax
from jax.experimental import pallas as pl
from jax.experimental.pallas import tpu as pltpu
from jax.sharding import PartitionSpec as P


PIX = 16
LANES = 8
GROUP = 8
ROWS = 16


def power_fit(values, nodes, degree):
    fit = np.polynomial.chebyshev.Chebyshev.fit(nodes, values, degree, domain=[0, 0.25])
    return [float(c) for c in fit.convert(kind=np.polynomial.Polynomial).coef]


def half_turn_fits():
    nodes = 0.125 * (1.0 - np.cos(np.pi * (np.arange(200) + 0.5) / 200))
    r = np.sqrt(nodes)
    root = math.sqrt(2.0)
    return (
        power_fit(root * np.sin(np.pi * r) / r, nodes, 3),
        power_fit(root * np.cos(np.pi * r), nodes, 3),
    )


SIN_FIT, COS_FIT = half_turn_fits()


def horner(coefs, z):
    value = z * coefs[-1] + coefs[-2]
    for c in coefs[-3::-1]:
        value = value * z + c
    return value


def cos_sin(phase):
    turns = phase * (1.0 / (2.0 * math.pi))
    r = turns - jnp.round(turns)
    z = r * r
    half_sin = horner(SIN_FIT, z) * r
    half_cos = horner(COS_FIT, z)
    return 1.0 - half_sin * half_sin, half_sin * half_cos


def dft_table(samples, pixels):
    freqs = np.arange(pixels) - pixels / 2.0
    table = np.exp(-2j * np.pi * freqs[:, None] * np.arange(samples)[None, :] / (2.0 * samples))
    full = np.kron(table, table)
    return np.concatenate([full.real, full.imag]).astype(np.float32)


def bf16_term(commands, slab):
    term = jnp.dot(commands, slab, preferred_element_type=jnp.float32)
    return term.astype(jnp.bfloat16).astype(jnp.float32)


def turned(ref_value):
    return ref_value.astype(jnp.float32).T.astype(jnp.bfloat16)


def prepare_kernel(
    mask_ref, cmds_ref, near_ref, amp_ref, abe_ref, table_ref, influence, trans_ref, phase_ref, valid_ref, field, own_slab, cmds, arrival
):
    subs, flat = trans_ref.shape[0], trans_ref.shape[2]
    half = trans_ref.shape[1] // 2
    fetch = pltpu.make_async_copy(influence.at[1], own_slab, arrival)
    fetch.start()
    cosine, sine = cos_sin(abe_ref[...])
    field[0] = (amp_ref[...] * cosine).T
    field[1] = (amp_ref[...] * sine).T
    row = lax.broadcasted_iota(jnp.int32, valid_ref.shape, 0)
    valid = jnp.zeros(valid_ref.shape, jnp.float32)
    for s in range(subs):
        valid = jnp.where(row == s, mask_ref[s].astype(jnp.float32), valid)
    valid_ref[...] = valid
    cmds[0] = turned(cmds_ref[...])
    cmds[1] = turned(near_ref[:, subs * flat :])

    def fold(s, carry):
        real, imag = field[0, pl.ds(s, 1), :], field[1, pl.ds(s, 1), :]
        real = jnp.broadcast_to(real, (PIX, flat))
        imag = jnp.broadcast_to(imag, (PIX, flat))
        for row in range(0, half, PIX):
            upper, lower = table_ref[row : row + PIX], table_ref[half + row : half + row + PIX]
            trans_ref[s, 2 * row : 2 * row + PIX] = (upper * real - lower * imag).astype(jnp.bfloat16)
            trans_ref[s, 2 * row + PIX : 2 * row + 2 * PIX] = (lower * real + upper * imag).astype(jnp.bfloat16)
        return carry

    lax.fori_loop(0, subs, fold, 0)
    fetch.wait()

    def add_terms(g, carry):
        for k in range(GROUP):
            s = g * GROUP + k
            cols = pl.ds(pl.multiple_of(s * flat, flat), flat)
            phase_ref[s] = bf16_term(cmds[0], own_slab[:, cols]) + bf16_term(cmds[1], near_ref[:, cols])
        return carry

    lax.fori_loop(0, subs // GROUP, add_terms, 0)


def prepare(mask, commands, near_sent, influence, amplitude, aberration):
    subs, samples = amplitude.shape[0], amplitude.shape[1]
    flat = samples * samples
    acts, patterns = commands.shape
    table = jnp.asarray(dft_table(samples, PIX))
    half = table.shape[0]
    whole = pl.BlockSpec(memory_space=pltpu.VMEM)
    return pl.pallas_call(
        prepare_kernel,
        in_specs=[pl.BlockSpec(memory_space=pltpu.SMEM)] + [whole] * 5 + [pl.BlockSpec(memory_space=pltpu.HBM)],
        out_specs=[whole] * 3,
        out_shape=[
            jax.ShapeDtypeStruct((subs, half, flat), jnp.bfloat16),
            jax.ShapeDtypeStruct((subs, patterns, flat), jnp.float32),
            jax.ShapeDtypeStruct((subs, patterns), jnp.float32),
        ],
        scratch_shapes=[
            pltpu.VMEM((2, subs, flat), jnp.float32),
            pltpu.VMEM((acts, subs * flat), jnp.bfloat16),
            pltpu.VMEM((2, patterns, acts), jnp.bfloat16),
            pltpu.SemaphoreType.DMA,
        ],
        compiler_params=pltpu.CompilerParams(vmem_limit_bytes=8 << 20),
        cost_estimate=pl.CostEstimate(flops=10**9, bytes_accessed=8 << 20, transcendentals=0),
        name="prepare",
    )(
        mask,
        commands,
        near_sent,
        amplitude.reshape(subs, flat).T,
        aberration.reshape(subs, flat).T,
        table,
        influence,
    )


def advance(running, pairs):
    (even_low, odd_low), (even_high, odd_high) = pairs
    if running is None:
        return (even_low, even_high, None), (odd_low, odd_high, None)
    found = []
    for (low, high, steps), more_low, more_high in zip(running, (even_low, odd_low), (even_high, odd_high)):
        both = low + high
        found.append((low + more_low, high + more_high, both if steps is None else steps + both))
    return found


def moments_of(low, high, steps):
    middle = (PIX - 1) / 2.0
    total = low + high
    row = lax.broadcasted_iota(jnp.int32, total.shape, 0).astype(jnp.float32)
    return total, total * middle - steps, low * (row - middle) + high * (row + (LANES - middle))


def spots_kernel(first, lead, done, valid_ref, cmds_ref, slab_ref, trans_ref, phase_ref, *refs):
    earlier, refs = refs[:done], refs[done:]
    out_ref, refs = refs[0], refs[1:]
    sums = refs[-1]
    flat = trans_ref.shape[2]
    patterns = out_ref.shape[2]
    count = sums.shape[2]
    size = math.gcd(count, GROUP)
    if lead:
        cmds = refs[0]
        cmds[...] = turned(cmds_ref[:, count * flat :])
    else:
        cmds = cmds_ref

    def group(g, carry):
        for k in range(size):
            s = g * size + k
            cols = pl.ds(pl.multiple_of(s * flat, flat), flat)
            term = jnp.dot(cmds[...], slab_ref[:, cols], preferred_element_type=jnp.float32)
            pieces = []
            for row in range(0, patterns, ROWS):
                part = term[row : row + ROWS].astype(jnp.bfloat16).astype(jnp.float32)
                phase = phase_ref[first + s, row : row + ROWS] + part
                pieces.append([w.astype(jnp.bfloat16) for w in cos_sin(phase)])
            waves = jnp.concatenate([p[0] for p in pieces] + [p[1] for p in pieces], axis=0)
            focal = lax.dot_general(
                trans_ref[first + s],
                waves,
                (((1,), (1,)), ((), ())),
                preferred_element_type=jnp.float32,
            )
            lines = focal.reshape(PIX, 2, PIX // LANES, LANES, 2 * patterns)
            running = None
            for u in range(PIX):
                pairs = []
                for v in range(PIX // LANES):
                    ur, vr = lines[u, 0, v, :, :patterns], lines[u, 0, v, :, patterns:]
                    ui, vi = lines[u, 1, v, :, :patterns], lines[u, 1, v, :, patterns:]
                    pairs.append(((ur * ur + ui * ui) + (vr * vr + vi * vi), ui * vr - ur * vi))
                running = advance(running, pairs)
            for kind, state in enumerate(running):
                for m, value in enumerate(moments_of(*state)):
                    sums[kind, m, s] = value
        return carry

    lax.fori_loop(0, count // size, group, 0)
    total = jnp.sum(sums[...], axis=3)
    even, odd = total[0], 2.0 * total[1]
    scale = 1.0 / ((even[0] + odd[0]) * (even[0] - odd[0]))
    scale = scale * valid_ref[first : first + count]
    for c in range(2):
        slope = ((odd[1 + c] * even[0] - even[1 + c] * odd[0]) * scale).astype(out_ref.dtype)
        pieces = [ref[c] for ref in earlier] + [slope]
        out_ref[c] = jnp.concatenate(pieces, axis=0) if earlier else slope


def spot_slopes(valid, cmds, slab, transform, phase, first, count, earlier):
    acts = slab.shape[0]
    patterns = phase.shape[1]
    lead = cmds is None
    rows = count + sum(part.shape[1] for part in earlier)
    whole = pl.BlockSpec(memory_space=pltpu.VMEM)
    out_shape = [jax.ShapeDtypeStruct((2, rows, patterns), jnp.bfloat16)]
    if lead:
        out_shape.append(jax.ShapeDtypeStruct((patterns, acts), jnp.bfloat16))
    return pl.pallas_call(
        lambda *refs: spots_kernel(first, lead, len(earlier), *refs),
        in_specs=[whole] * (5 + len(earlier)),
        out_specs=[whole] * len(out_shape),
        out_shape=out_shape,
        scratch_shapes=[pltpu.VMEM((2, 3, count, LANES, patterns), jnp.float32)],
        compiler_params=pltpu.CompilerParams(vmem_limit_bytes=8 << 20),
        cost_estimate=pl.CostEstimate(flops=10**8 * count, bytes_accessed=10**6, transcendentals=0),
        name="spots",
    )(valid, slab if lead else cmds, slab, transform, phase, *earlier)


def decode_kernel(signs_ref, stroke_ref, same_ref, other_ref, out_ref):
    pairs, rows, patterns = same_ref.shape
    acts = signs_ref.shape[0]
    subs = rows // 2
    signs = signs_ref[...].astype(jnp.float32).astype(jnp.bfloat16)
    scale = jnp.broadcast_to(1.0 / (stroke_ref[...] * patterns), (LANES, acts)).T[:, :1]

    def write(even_ref, odd_ref):
        for c in range(2):
            part = slice(c * subs, (c + 1) * subs)
            slopes = jnp.stack([even_ref[:, part, :], odd_ref[:, part, :]], axis=1)
            summed = lax.dot_general(
                signs,
                slopes.reshape(2 * pairs * subs, patterns),
                (((1,), (1,)), ((), ())),
                preferred_element_type=jnp.float32,
            )
            out_ref[:, c, :] = summed * scale

    parity = tile_parity()
    pl.when(parity == 0)(lambda: write(same_ref, other_ref))
    pl.when(parity == 1)(lambda: write(other_ref, same_ref))


def decode(signs, stroke, same, other):
    pairs, rows, _ = same.shape
    acts = signs.shape[0]
    return pl.pallas_call(
        decode_kernel,
        in_specs=[pl.BlockSpec(memory_space=pltpu.VMEM)] * 4,
        out_specs=pl.BlockSpec(memory_space=pltpu.VMEM),
        out_shape=jax.ShapeDtypeStruct((acts, 2, pairs * rows), jnp.float32),
        compiler_params=pltpu.CompilerParams(vmem_limit_bytes=8 << 20),
        name="decode",
    )(signs, stroke.reshape(1, acts), same, other)


def tile_parity():
    return lax.rem(lax.axis_index("tile"), 2)


def in_hbm(value):
    return pltpu.with_memory_space_constraint(value, pltpu.HBM)


def pack_first_kernel(signs_hbm, stroke_hbm, influence, sent_ref, cmds_ref, signs, stroke, arrivals):
    acts, patterns = cmds_ref.shape
    width = sent_ref.shape[1] - patterns
    far_row = 2 * tile_parity()
    moves = (
        (signs_hbm, signs),
        (stroke_hbm, stroke),
        (influence.at[far_row, :, pl.ds(0, width)], sent_ref.at[:, pl.ds(0, width)]),
    )
    fetches = [pltpu.make_async_copy(*move, arrivals.at[k]) for k, move in enumerate(moves)]
    for fetch in fetches:
        fetch.start()
    fetches[0].wait()
    fetches[1].wait()
    column = jnp.broadcast_to(stroke[...][None, :], (LANES, acts)).T[:, :1]
    commands = (column * signs[...].astype(jnp.float32)).astype(jnp.bfloat16)
    cmds_ref[...] = commands
    sent_ref[:, width:] = commands
    fetches[2].wait()


def pack_first(signs, stroke, influence, width):
    acts, patterns = signs.shape
    whole, far_off = pl.BlockSpec(memory_space=pltpu.VMEM), pl.BlockSpec(memory_space=pltpu.HBM)
    return pl.pallas_call(
        pack_first_kernel,
        in_specs=[far_off] * 3,
        out_specs=[whole] * 2,
        out_shape=[
            jax.ShapeDtypeStruct((acts, width + patterns), jnp.bfloat16),
            jax.ShapeDtypeStruct((acts, patterns), jnp.bfloat16),
        ],
        scratch_shapes=[
            pltpu.VMEM((acts, patterns), jnp.int32),
            pltpu.VMEM((acts,), jnp.float32),
            pltpu.SemaphoreType.DMA((3,)),
        ],
        compiler_params=pltpu.CompilerParams(vmem_limit_bytes=8 << 20),
        name="pack_first",
    )(signs, stroke, influence)


def pack_rest_kernel(cmds_ref, influence, *refs):
    pieces, near_ref, arrivals = refs[:-2], refs[-2], refs[-1]
    points = influence.shape[2]
    far_row = 2 * tile_parity()
    near_row = 2 - far_row
    fetches = [
        pltpu.make_async_copy(influence.at[near_row], near_ref.at[:, pl.ds(0, points)], arrivals.at[0])
    ]
    first = points - sum(ref.shape[1] for ref in pieces)
    for k, ref in enumerate(pieces):
        source = influence.at[far_row, :, pl.ds(first, ref.shape[1])]
        fetches.append(pltpu.make_async_copy(source, ref, arrivals.at[k + 1]))
        first += ref.shape[1]
    for fetch in fetches:
        fetch.start()
    near_ref[:, points:] = cmds_ref[...]
    for fetch in fetches:
        fetch.wait()


def pack_rest(commands, influence, widths):
    acts, patterns = commands.shape
    whole = pl.BlockSpec(memory_space=pltpu.VMEM)
    shapes = [(acts, width) for width in widths] + [(acts, influence.shape[2] + patterns)]
    return pl.pallas_call(
        pack_rest_kernel,
        in_specs=[whole, pl.BlockSpec(memory_space=pltpu.HBM)],
        out_specs=[whole] * len(shapes),
        out_shape=[jax.ShapeDtypeStruct(shape, jnp.bfloat16) for shape in shapes],
        scratch_shapes=[pltpu.SemaphoreType.DMA((len(shapes),))],
        compiler_params=pltpu.CompilerParams(vmem_limit_bytes=8 << 20),
        name="pack_rest",
    )(commands, influence)


def pairings(count):
    near = [(i, i ^ 1) for i in range(count) if (i ^ 1) < count]
    far = [(i, i + 1 if i % 2 else i - 1) for i in range(count)]
    return near, [(a, b) for a, b in far if 0 <= b < count]


def chunk_sizes(subs):
    unit = subs // 8
    return [k * unit for k in (2, 2, 2, 1, 1)]


def interaction(hadamard, stroke, influence, amplitude, aberration, valid_mask):
    count = lax.axis_size("tile")
    subs = amplitude.shape[0]
    flat = influence.shape[2] // subs
    near, far = pairings(count)
    influence = in_hbm(influence)
    sizes = chunk_sizes(subs)
    firsts = [sum(sizes[:k]) for k in range(len(sizes))]
    widths = [size * flat for size in sizes]
    first_sent, commands = pack_first(in_hbm(hadamard.T), in_hbm(stroke), influence, widths[0])
    far_slabs = [lax.ppermute(first_sent, "tile", far)]
    *rest, near_slab = pack_rest(commands, influence, widths[1:])
    near_sent = lax.ppermute(near_slab, "tile", near)
    for piece in rest:
        far_slabs.append(lax.ppermute(piece, "tile", far))
    transform, phase, valid = prepare(valid_mask, commands, near_sent, influence, amplitude, aberration)
    parts, far_cmds = [], None
    for k, (first, size) in enumerate(zip(firsts, sizes)):
        earlier = parts[-1:]
        found = spot_slopes(valid, far_cmds, far_slabs[k], transform, phase, first, size, earlier)
        parts.append(found[0])
        if k == 0:
            far_cmds = found[1]
    slopes = parts[-1].reshape(2 * subs, -1)
    groups = [list(range(side, count, 2)) for side in range(2)]
    copies = jnp.broadcast_to(slopes, (count // 2, *slopes.shape))
    same = lax.all_to_all(copies, "tile", 0, 0, axis_index_groups=groups)
    other = lax.ppermute(same, "tile", near)
    return decode(hadamard.T, stroke, same, other)


def solution(mesh):
    placed = (
        P(None, "tile"),
        P(("group", "tile")),
        P(None, ("group", "tile"), None),
        P(("group", "tile"), None, None),
        P(("group", "tile"), None, None),
        P(("group", "tile")),
    )
    return jax.shard_map(
        interaction,
        mesh=mesh,
        in_specs=placed,
        out_specs=P(("group", "tile"), None, None),
        check_vma=False,
    )
```

```python
import math

import jax
import jax.numpy as jnp
import numpy as np
from jax import lax
from jax.experimental import pallas as pl
from jax.experimental.pallas import tpu as pltpu
from jax.sharding import PartitionSpec as P


PIX = 16
LANES = 8
GROUP = 8
ROWS = 16


def power_fit(values, nodes, degree):
    fit = np.polynomial.chebyshev.Chebyshev.fit(nodes, values, degree, domain=[0, 0.25])
    return [float(c) for c in fit.convert(kind=np.polynomial.Polynomial).coef]


def half_turn_fits():
    nodes = 0.125 * (1.0 - np.cos(np.pi * (np.arange(200) + 0.5) / 200))
    r = np.sqrt(nodes)
    root = math.sqrt(2.0)
    return (
        power_fit(root * np.sin(np.pi * r) / r, nodes, 3),
        power_fit(root * np.cos(np.pi * r), nodes, 4),
    )


SIN_FIT, COS_FIT = half_turn_fits()


def horner(coefs, z):
    value = z * coefs[-1] + coefs[-2]
    for c in coefs[-3::-1]:
        value = value * z + c
    return value


def cos_sin(phase):
    turns = phase * (1.0 / (2.0 * math.pi))
    r = turns - jnp.round(turns)
    z = r * r
    half_sin = horner(SIN_FIT, z) * r
    half_cos = horner(COS_FIT, z)
    return 1.0 - half_sin * half_sin, half_sin * half_cos


def dft_table(samples, pixels):
    freqs = np.arange(pixels) - pixels / 2.0
    table = np.exp(-2j * np.pi * freqs[:, None] * np.arange(samples)[None, :] / (2.0 * samples))
    full = np.kron(table, table)
    return np.concatenate([full.real, full.imag]).astype(np.float32)


def bf16_term(commands, slab):
    term = jnp.dot(commands, slab, preferred_element_type=jnp.float32)
    return term.astype(jnp.bfloat16).astype(jnp.float32)


def turned(ref_value):
    return ref_value.astype(jnp.float32).T.astype(jnp.bfloat16)


def prepare_kernel(
    mask_ref, cmds_ref, near_ref, amp_ref, abe_ref, table_ref, influence, trans_ref, phase_ref, valid_ref, field, own_slab, cmds, arrival
):
    subs, flat = trans_ref.shape[0], trans_ref.shape[2]
    half = trans_ref.shape[1] // 2
    fetch = pltpu.make_async_copy(influence.at[1], own_slab, arrival)
    fetch.start()
    cosine, sine = cos_sin(abe_ref[...])
    field[0] = (amp_ref[...] * cosine).T
    field[1] = (amp_ref[...] * sine).T
    row = lax.broadcasted_iota(jnp.int32, valid_ref.shape, 0)
    valid = jnp.zeros(valid_ref.shape, jnp.float32)
    for s in range(subs):
        valid = jnp.where(row == s, mask_ref[s].astype(jnp.float32), valid)
    valid_ref[...] = valid
    cmds[0] = turned(cmds_ref[...])
    cmds[1] = turned(near_ref[:, subs * flat :])

    def fold(s, carry):
        real, imag = field[0, pl.ds(s, 1), :], field[1, pl.ds(s, 1), :]
        real = jnp.broadcast_to(real, (PIX, flat))
        imag = jnp.broadcast_to(imag, (PIX, flat))
        for row in range(0, half, PIX):
            upper, lower = table_ref[row : row + PIX], table_ref[half + row : half + row + PIX]
            trans_ref[s, 2 * row : 2 * row + PIX] = (upper * real - lower * imag).astype(jnp.bfloat16)
            trans_ref[s, 2 * row + PIX : 2 * row + 2 * PIX] = (lower * real + upper * imag).astype(jnp.bfloat16)
        return carry

    lax.fori_loop(0, subs, fold, 0, unroll=4)
    fetch.wait()

    def add_terms(g, carry):
        for k in range(GROUP):
            s = g * GROUP + k
            cols = pl.ds(pl.multiple_of(s * flat, flat), flat)
            phase_ref[s] = bf16_term(cmds[0], own_slab[:, cols]) + bf16_term(cmds[1], near_ref[:, cols])
        return carry

    lax.fori_loop(0, subs // GROUP, add_terms, 0)


def prepare(mask, commands, near_sent, influence, amplitude, aberration):
    subs, samples = amplitude.shape[0], amplitude.shape[1]
    flat = samples * samples
    acts, patterns = commands.shape
    table = jnp.asarray(dft_table(samples, PIX))
    half = table.shape[0]
    whole = pl.BlockSpec(memory_space=pltpu.VMEM)
    return pl.pallas_call(
        prepare_kernel,
        in_specs=[pl.BlockSpec(memory_space=pltpu.SMEM)] + [whole] * 5 + [pl.BlockSpec(memory_space=pltpu.HBM)],
        out_specs=[whole] * 3,
        out_shape=[
            jax.ShapeDtypeStruct((subs, half, flat), jnp.bfloat16),
            jax.ShapeDtypeStruct((subs, patterns, flat), jnp.float32),
            jax.ShapeDtypeStruct((subs, patterns), jnp.float32),
        ],
        scratch_shapes=[
            pltpu.VMEM((2, subs, flat), jnp.float32),
            pltpu.VMEM((acts, subs * flat), jnp.bfloat16),
            pltpu.VMEM((2, patterns, acts), jnp.bfloat16),
            pltpu.SemaphoreType.DMA,
        ],
        compiler_params=pltpu.CompilerParams(vmem_limit_bytes=8 << 20),
        cost_estimate=pl.CostEstimate(flops=10**9, bytes_accessed=8 << 20, transcendentals=0),
        name="prepare",
    )(
        mask,
        commands,
        near_sent,
        amplitude.reshape(subs, flat).T,
        aberration.reshape(subs, flat).T,
        table,
        influence,
    )


def advance(running, pairs):
    (even_low, odd_low), (even_high, odd_high) = pairs
    if running is None:
        return (even_low, even_high, None), (odd_low, odd_high, None)
    found = []
    for (low, high, steps), more_low, more_high in zip(running, (even_low, odd_low), (even_high, odd_high)):
        both = low + high
        found.append((low + more_low, high + more_high, both if steps is None else steps + both))
    return found


def moments_of(low, high, steps):
    middle = (PIX - 1) / 2.0
    total = low + high
    row = lax.broadcasted_iota(jnp.int32, total.shape, 0).astype(jnp.float32)
    return total, total * middle - steps, low * (row - middle) + high * (row + (LANES - middle))


def spots_kernel(first, lead, done, valid_ref, cmds_ref, slab_ref, trans_ref, phase_ref, *refs):
    earlier, refs = refs[:done], refs[done:]
    out_ref, refs = refs[0], refs[1:]
    sums = refs[-1]
    flat = trans_ref.shape[2]
    patterns = out_ref.shape[2]
    count = sums.shape[2]
    size = math.gcd(count, GROUP)
    if lead:
        cmds = refs[0]
        cmds[...] = turned(cmds_ref[:, count * flat :])
    else:
        cmds = cmds_ref

    def group(g, carry):
        for k in range(size):
            s = g * size + k
            cols = pl.ds(pl.multiple_of(s * flat, flat), flat)
            term = jnp.dot(cmds[...], slab_ref[:, cols], preferred_element_type=jnp.float32)
            pieces = []
            for row in range(0, patterns, ROWS):
                part = term[row : row + ROWS].astype(jnp.bfloat16).astype(jnp.float32)
                phase = phase_ref[first + s, row : row + ROWS] + part
                pieces.append([w.astype(jnp.bfloat16) for w in cos_sin(phase)])
            waves = jnp.concatenate([p[0] for p in pieces] + [p[1] for p in pieces], axis=0)
            focal = lax.dot_general(
                trans_ref[first + s],
                waves,
                (((1,), (1,)), ((), ())),
                preferred_element_type=jnp.float32,
            )
            lines = focal.reshape(PIX, 2, PIX // LANES, LANES, 2 * patterns)
            running = None
            for u in range(PIX):
                pairs = []
                for v in range(PIX // LANES):
                    ur, vr = lines[u, 0, v, :, :patterns], lines[u, 0, v, :, patterns:]
                    ui, vi = lines[u, 1, v, :, :patterns], lines[u, 1, v, :, patterns:]
                    pairs.append(((ur * ur + ui * ui) + (vr * vr + vi * vi), ui * vr - ur * vi))
                running = advance(running, pairs)
            for kind, state in enumerate(running):
                for m, value in enumerate(moments_of(*state)):
                    sums[kind, m, s] = value
        return carry

    lax.fori_loop(0, count // size, group, 0)
    total = jnp.sum(sums[...], axis=3)
    even, odd = total[0], 2.0 * total[1]
    scale = 1.0 / ((even[0] + odd[0]) * (even[0] - odd[0]))
    scale = scale * valid_ref[first : first + count]
    for c in range(2):
        slope = ((odd[1 + c] * even[0] - even[1 + c] * odd[0]) * scale).astype(out_ref.dtype)
        pieces = [ref[c] for ref in earlier] + [slope]
        out_ref[c] = jnp.concatenate(pieces, axis=0) if earlier else slope


def spot_slopes(valid, cmds, slab, transform, phase, first, count, earlier):
    acts = slab.shape[0]
    patterns = phase.shape[1]
    lead = cmds is None
    rows = count + sum(part.shape[1] for part in earlier)
    whole = pl.BlockSpec(memory_space=pltpu.VMEM)
    out_shape = [jax.ShapeDtypeStruct((2, rows, patterns), jnp.bfloat16)]
    if lead:
        out_shape.append(jax.ShapeDtypeStruct((patterns, acts), jnp.bfloat16))
    return pl.pallas_call(
        lambda *refs: spots_kernel(first, lead, len(earlier), *refs),
        in_specs=[whole] * (5 + len(earlier)),
        out_specs=[whole] * len(out_shape),
        out_shape=out_shape,
        scratch_shapes=[pltpu.VMEM((2, 3, count, LANES, patterns), jnp.float32)],
        compiler_params=pltpu.CompilerParams(vmem_limit_bytes=8 << 20),
        cost_estimate=pl.CostEstimate(flops=10**8 * count, bytes_accessed=10**6, transcendentals=0),
        name="spots",
    )(valid, slab if lead else cmds, slab, transform, phase, *earlier)


def decode_kernel(signs_ref, stroke_ref, same_ref, other_ref, out_ref):
    pairs, rows, patterns = same_ref.shape
    acts = signs_ref.shape[0]
    subs = rows // 2
    signs = signs_ref[...].astype(jnp.float32).astype(jnp.bfloat16)
    scale = jnp.broadcast_to(1.0 / (stroke_ref[...] * patterns), (LANES, acts)).T[:, :1]

    def write(outer_ref, inner_ref):
        for c in range(2):
            part = slice(c * subs, (c + 1) * subs)
            pieces = []
            for k in range(pairs):
                ends = [outer_ref[k, part, :], inner_ref[k, part, :]]
                pieces += ends if k % 2 == 0 else ends[::-1]
            summed = lax.dot_general(
                signs,
                jnp.concatenate(pieces, axis=0),
                (((1,), (1,)), ((), ())),
                preferred_element_type=jnp.float32,
            )
            out_ref[:, c, :] = summed * scale

    side = tile_side()
    pl.when(side == 0)(lambda: write(same_ref, other_ref))
    pl.when(side == 1)(lambda: write(other_ref, same_ref))


def decode(signs, stroke, same, other):
    pairs, rows, _ = same.shape
    acts = signs.shape[0]
    return pl.pallas_call(
        decode_kernel,
        in_specs=[pl.BlockSpec(memory_space=pltpu.VMEM)] * 4,
        out_specs=pl.BlockSpec(memory_space=pltpu.VMEM),
        out_shape=jax.ShapeDtypeStruct((acts, 2, pairs * rows), jnp.float32),
        compiler_params=pltpu.CompilerParams(vmem_limit_bytes=8 << 20),
        name="decode",
    )(signs, stroke.reshape(1, acts), same, other)


def tile_parity():
    return lax.rem(lax.axis_index("tile"), 2)


def tile_side():
    return lax.rem(lax.div(lax.axis_index("tile") + 1, 2), 2)


def in_hbm(value):
    return pltpu.with_memory_space_constraint(value, pltpu.HBM)


def pack_first_kernel(signs_hbm, stroke_hbm, influence, sent_ref, cmds_ref, signs, stroke, arrivals):
    acts, patterns = cmds_ref.shape
    width = sent_ref.shape[1] - patterns
    far_row = 2 * tile_parity()
    moves = (
        (signs_hbm, signs),
        (stroke_hbm, stroke),
        (influence.at[far_row, :, pl.ds(0, width)], sent_ref.at[:, pl.ds(0, width)]),
    )
    fetches = [pltpu.make_async_copy(*move, arrivals.at[k]) for k, move in enumerate(moves)]
    for fetch in fetches:
        fetch.start()
    fetches[0].wait()
    fetches[1].wait()
    column = jnp.broadcast_to(stroke[...][None, :], (LANES, acts)).T[:, :1]
    commands = (column * signs[...].astype(jnp.float32)).astype(jnp.bfloat16)
    cmds_ref[...] = commands
    sent_ref[:, width:] = commands
    fetches[2].wait()


def pack_first(signs, stroke, influence, width):
    acts, patterns = signs.shape
    whole, far_off = pl.BlockSpec(memory_space=pltpu.VMEM), pl.BlockSpec(memory_space=pltpu.HBM)
    return pl.pallas_call(
        pack_first_kernel,
        in_specs=[far_off] * 3,
        out_specs=[whole] * 2,
        out_shape=[
            jax.ShapeDtypeStruct((acts, width + patterns), jnp.bfloat16),
            jax.ShapeDtypeStruct((acts, patterns), jnp.bfloat16),
        ],
        scratch_shapes=[
            pltpu.VMEM((acts, patterns), jnp.int32),
            pltpu.VMEM((acts,), jnp.float32),
            pltpu.SemaphoreType.DMA((3,)),
        ],
        compiler_params=pltpu.CompilerParams(vmem_limit_bytes=8 << 20),
        name="pack_first",
    )(signs, stroke, influence)


def pack_rest_kernel(cmds_ref, influence, *refs):
    pieces, near_ref, arrivals = refs[:-2], refs[-2], refs[-1]
    points = influence.shape[2]
    far_row = 2 * tile_parity()
    near_row = 2 - far_row
    fetches = [
        pltpu.make_async_copy(influence.at[near_row], near_ref.at[:, pl.ds(0, points)], arrivals.at[0])
    ]
    first = points - sum(ref.shape[1] for ref in pieces)
    for k, ref in enumerate(pieces):
        source = influence.at[far_row, :, pl.ds(first, ref.shape[1])]
        fetches.append(pltpu.make_async_copy(source, ref, arrivals.at[k + 1]))
        first += ref.shape[1]
    for fetch in fetches:
        fetch.start()
    near_ref[:, points:] = cmds_ref[...]
    for fetch in fetches:
        fetch.wait()


def pack_rest(commands, influence, widths):
    acts, patterns = commands.shape
    whole = pl.BlockSpec(memory_space=pltpu.VMEM)
    shapes = [(acts, width) for width in widths] + [(acts, influence.shape[2] + patterns)]
    return pl.pallas_call(
        pack_rest_kernel,
        in_specs=[whole, pl.BlockSpec(memory_space=pltpu.HBM)],
        out_specs=[whole] * len(shapes),
        out_shape=[jax.ShapeDtypeStruct(shape, jnp.bfloat16) for shape in shapes],
        scratch_shapes=[pltpu.SemaphoreType.DMA((len(shapes),))],
        compiler_params=pltpu.CompilerParams(vmem_limit_bytes=8 << 20),
        name="pack_rest",
    )(commands, influence)


def pairings(count):
    near = [(i, i ^ 1) for i in range(count) if (i ^ 1) < count]
    far = [(i, i + 1 if i % 2 else i - 1) for i in range(count)]
    return near, [(a, b) for a, b in far if 0 <= b < count]


def chunk_sizes(subs):
    unit = subs // 8
    return [k * unit for k in (2, 2, 2, 1, 1)]


def interaction(hadamard, stroke, influence, amplitude, aberration, valid_mask):
    count = lax.axis_size("tile")
    subs = amplitude.shape[0]
    flat = influence.shape[2] // subs
    near, far = pairings(count)
    influence = in_hbm(influence)
    sizes = chunk_sizes(subs)
    firsts = [sum(sizes[:k]) for k in range(len(sizes))]
    widths = [size * flat for size in sizes]
    first_sent, commands = pack_first(in_hbm(hadamard.T), in_hbm(stroke), influence, widths[0])
    far_slabs = [lax.ppermute(first_sent, "tile", far)]
    *rest, near_slab = pack_rest(commands, influence, widths[1:])
    near_sent = lax.ppermute(near_slab, "tile", near)
    for piece in rest:
        far_slabs.append(lax.ppermute(piece, "tile", far))
    transform, phase, valid = prepare(valid_mask, commands, near_sent, influence, amplitude, aberration)
    parts, far_cmds = [], None
    for k, (first, size) in enumerate(zip(firsts, sizes)):
        earlier = parts[-1:]
        found = spot_slopes(valid, far_cmds, far_slabs[k], transform, phase, first, size, earlier)
        parts.append(found[0])
        if k == 0:
            far_cmds = found[1]
    slopes = parts[-1].reshape(2 * subs, -1)
    groups = [[t for t in range(count) if (t + 1) // 2 % 2 == side] for side in range(2)]
    copies = jnp.broadcast_to(slopes, (count // 2, *slopes.shape))
    same = lax.all_to_all(copies, "tile", 0, 0, axis_index_groups=groups)
    other = lax.ppermute(same, "tile", near)
    return decode(hadamard.T, stroke, same, other)


def solution(mesh):
    placed = (
        P(None, "tile"),
        P(("group", "tile")),
        P(None, ("group", "tile"), None),
        P(("group", "tile"), None, None),
        P(("group", "tile"), None, None),
        P(("group", "tile")),
    )
    return jax.shard_map(
        interaction,
        mesh=mesh,
        in_specs=placed,
        out_specs=P(("group", "tile"), None, None),
        check_vma=False,
    )
```
